32 devices in a mesh: section: 2 (over core), fsdp: 4 (over z), dp: 4 (over y, x).
Axes of the slice: x: 2, y: 2, z: 4, core: 2. Of those that a mesh axis runs over, the one named last changes fastest.
Arguments:
- tokens: bfloat16 [1, 16, 128, 1024], P(None, ('fsdp', 'dp')), may hold values from -6 to 6
- segments: int32 [1, 16, 128], P(None, ('fsdp', 'dp')), may hold values from 0 to 3, never falling along the last dimension, each value on 1 to 64 neighbouring positions
- cotangent: float32 [1, 16, 128, 1024], P(None, ('fsdp', 'dp')), may hold values from -6 to 6
- norm_gains: bfloat16 [2, 2, 1024], P('section', None, 'fsdp'), may hold values from 0.5 to 1.5
- proj_weight: bfloat16 [2, 1024, 3072], P('section', 'fsdp'), may hold values from -0.1875 to 0.1875
- rate_weight: bfloat16 [2, 1024, 8], P('section', 'fsdp'), may hold values from -0.1875 to 0.1875
- out_weight: bfloat16 [2, 1024, 1024], P('section', 'fsdp'), may hold values from -0.375 to 0.375
- up_weight: bfloat16 [2, 1024, 5632], P('section', 'fsdp'), may hold values from -0.1875 to 0.1875
- down_weight: bfloat16 [2, 1024, 2816], P('section', 'fsdp'), may hold values from -0.21875 to 0.21875
- conv_kernels: float32 [2, 4, 2048], P('section'), may hold values from -3 to 3
- head_params: float32 [2, 2, 4], P('section'), may hold values from -2.5 to 0.5
- out_gain: float32 [2, 256], P('section'), may hold values from 0.5 to 1.5
Outputs:
- section_output: bfloat16 [2, 1, 16, 128, 1024], P('section', None, ('fsdp', 'dp'))
- input_grad: float32 [2, 1, 16, 128, 1024], P('section', None, ('fsdp', 'dp'))
- gains_grad: float32 [2, 2, 1024], P('section', None, 'fsdp')
- proj_grad: float32 [2, 1024, 3072], P('section', 'fsdp')
- rate_grad: float32 [2, 1024, 8], P('section', 'fsdp')
- out_grad: float32 [2, 1024, 1024], P('section', 'fsdp')
- up_grad: float32 [2, 1024, 5632], P('section', 'fsdp')
- down_grad: float32 [2, 1024, 2816], P('section', 'fsdp')
- kernel_grad: float32 [2, 4, 2048], P('section')
- head_grad: float32 [2, 2, 4], P('section')
- out_gain_grad: float32 [2, 256], P('section')
The draws below stay inside these ranges and needn't reach their ends.
Inputs may be any that keep to these rules, and one draw needn't show every extreme that they name: `segments`: within each sequence the numbers never fall, every one of 0 .. 3 occurs, and each document holds 1 to 64 positions, one exactly 64.
All inputs are finite; a program needn't handle non-finite values.
Results may differ from the reference program's by a relative error of at most 0.034.
Values may be sent and summed in bfloat16 or wider, within the bound.
A program may use at most 256 MiB of HBM per device.

```python
import math
from functools import partial
import jax
import jax.numpy as jnp
import numpy as np
from jax import lax

D = 1024
H = 4
DK = 128
DV = 256
FF = 2816
CONV = 4
SPAN = 64
DOCS = 4
MB = 1
SEQ = 128
SEQS = 16


def block_levels(key, extent, shards, least, high):
    level, own = 1.0, jax.random.fold_in(key, 6)
    for dim, shards_of in shards:
        steps = jnp.exp(jax.random.uniform(jax.random.fold_in(own, dim), (shards_of,), jnp.float32, least / len(shards), high / len(shards)))
        level = level * jnp.repeat(steps, extent[dim] // shards_of).reshape([-1 if axis == dim else 1 for axis in range(len(extent))])
    return level


def split_up(count, total, reach, skew):
    loads = [(1 << 20) // math.isqrt(rank ** skew) + 1 for rank in range(2, count + 1)]
    spare, holding = total - reach - (count - 1), [1] * (count - 1)
    while spare > 0:
        candidates = [i for i in range(count - 1) if holding[i] < reach]
        mass, budget = sum([loads[i] for i in candidates]), spare
        for i in candidates:
            more = min(reach - holding[i], max(1, budget * loads[i] // mass), spare)
            holding[i] = holding[i] + more
            spare = spare - more
    return np.array([reach] + holding)


def uneven_parts(rng, amount, total, most, skew):
    if amount == 2:
        one = jax.random.randint(rng, (), max(1, total - most), min(most, total - 1) + 1)
        return jnp.stack([one, total - one])
    lengths = jnp.asarray(split_up(amount, total, most, skew), jnp.int32)
    couples = (amount - 1) // 2
    source_of, taker = lengths[1:1 + 2 * couples:2], lengths[2:2 + 2 * couples:2]
    slack = jnp.minimum(source_of - 1, most - taker)
    moved = jax.random.randint(jax.random.fold_in(rng, 1), (couples,), 0, 1 << 20) % (slack + 1)
    lengths = lengths.at[1:1 + 2 * couples:2].set(source_of - moved).at[2:2 + 2 * couples:2].set(taker + moved)
    return lengths[jax.random.permutation(jax.random.fold_in(rng, 2), amount)]


def centred(rng, shape, deviation, reach, split=(), kind=jnp.bfloat16):
    loudness = block_levels(rng, shape, split, -0.22, 0.18) if split else 1.0
    drawn = jax.random.normal(rng, shape, jnp.float32) * deviation * loudness
    return jnp.minimum(jnp.maximum(drawn, -reach), reach).astype(kind)


def setup_inputs(seed: int = 0) -> dict:
    streams_of = jax.random.split(jax.random.key(seed), 13)
    return {
        "tokens": centred(streams_of[0], (MB, SEQS, SEQ, D), 1.0, 6.0, ((1, 16),)),
        "segments": jax.vmap(lambda own: jnp.searchsorted(jnp.cumsum(uneven_parts(own, DOCS, SEQ, SEQ // 2, 1)), jnp.arange(SEQ), side="right"))(jax.random.split(streams_of[1], MB * SEQS)).reshape((MB, SEQS, SEQ)).astype(jnp.int32),
        "cotangent": centred(streams_of[2], (MB, SEQS, SEQ, D), 1.0, 6.0, ((1, 16),), jnp.float32),
        "norm_gains": jnp.clip(1.0 + 0.1 * jax.random.normal(streams_of[3], (2, 2, D), jnp.float32), 0.5, 1.5).astype(jnp.bfloat16),
        "proj_weight": centred(streams_of[4], (2, D, 2 * H * DK + 2 * H * DV), D ** -0.5, 0.1875, ((0, 2), (1, 4))),
        "rate_weight": centred(streams_of[5], (2, D, 2 * H), D ** -0.5, 0.1875, ((0, 2), (1, 4))),
        "out_weight": centred(streams_of[6], (2, D, H * DV), (H * DV // 4) ** -0.5, 0.375, ((0, 2), (1, 4))),
        "up_weight": centred(streams_of[7], (2, D, 2 * FF), D ** -0.5, 0.1875, ((0, 2), (1, 4))),
        "down_weight": centred(streams_of[8], (2, D, FF), (FF // 4) ** -0.5, 0.21875, ((0, 2), (1, 4))),
        "conv_kernels": centred(streams_of[9], (2, CONV, 2 * H * DK + H * DV), 0.5, 3.0, ((0, 2),), jnp.float32),
        "head_params": jnp.clip(-2.5 + 3.0 * jax.random.uniform(streams_of[10], (2, 2, H), jnp.float32) ** block_levels(streams_of[10], (2, 2, H), ((0, 2),), -0.2, 0.2), -2.5, 0.5),
        "out_gain": jnp.clip(1.0 + 0.1 * jax.random.normal(streams_of[11], (2, DV), jnp.float32), 0.5, 1.5),
    }


highest = lax.Precision.HIGHEST
reset_level = -30.0

def rms_gain(values, gain_vec):
    return values * lax.rsqrt(lax.optimization_barrier(jnp.mean(values * values, -1, keepdims=True)) + 1e-06) * gain_vec

def swiglu(joined):
    half_width = joined.shape[-1] // 2
    return jax.nn.silu(joined[..., :half_width]) * joined[..., half_width:]

def short_conv(raw_input, kernel, segment):
    length = raw_input.shape[1]
    tap_count = kernel.shape[0]
    total = raw_input * kernel[tap_count - 1]
    for offset in range(1, tap_count):
        shifted = jnp.pad(raw_input, ((0, 0), (offset, 0), (0, 0)))[:, :length]
        earlier = jnp.pad(segment, ((0, 0), (offset, 0)), constant_values=-1)[:, :length]
        total = total + jnp.where((earlier == segment)[..., None], shifted, 0.0) * kernel[tap_count - 1 - offset]
    return jax.nn.silu(total)

def delta_rule(queries, key_rows, value_rows, beta_gate, decays, block_len):
    batch_size, head_count, length, key_dim = queries.shape
    value_dim = value_rows.shape[-1]
    block_count = length // block_len

    def to_blocks(array):
        return array.reshape(array.shape[:2] + (block_count, block_len) + array.shape[3:])
    queries = to_blocks(queries)
    key_rows = to_blocks(key_rows)
    value_rows = to_blocks(value_rows)
    beta_gate = to_blocks(beta_gate)
    levels = jnp.cumsum(to_blocks(decays), axis=-1)
    places = jnp.arange(block_len)
    lower_mask = places[:, None] >= places[None, :]
    strict_mask = places[:, None] > places[None, :]
    spread = jnp.exp(jnp.where(lower_mask, levels[..., :, None] - levels[..., None, :], -1e+30))
    beta_keys = key_rows * beta_gate[..., None]
    key_inner = jnp.einsum('bhncd,bhnmd->bhncm', beta_keys, key_rows, precision=highest) * spread
    system = jnp.where(strict_mask, key_inner, 0.0)
    right_side = jnp.concatenate([beta_keys * jnp.exp(levels)[..., None], value_rows * beta_gate[..., None]], -1)
    solved = lax.linalg.triangular_solve(system, right_side, left_side=True, lower=True, unit_diagonal=True)
    solved_keys = solved[..., :key_dim]
    solved_values = solved[..., key_dim:]
    scores = jnp.einsum('bhncd,bhnmd->bhncm', queries, key_rows, precision=highest) * spread
    fading = queries * jnp.exp(levels)[..., None]
    final_level = levels[..., -1:]
    carried = key_rows * jnp.exp(final_level - levels)[..., None]

    def advance(memory, pieces):
        fading_part, keys_part, values_part, scores_part, carried_part, final_part = pieces
        update = values_part - jnp.einsum('bhcd,bhde->bhce', keys_part, memory, precision=highest)
        output = jnp.einsum('bhcd,bhde->bhce', fading_part, memory, precision=highest) + jnp.einsum('bhcm,bhme->bhce', scores_part, update, precision=highest)
        memory = memory * jnp.exp(final_part)[..., None] + jnp.einsum('bhcd,bhce->bhde', carried_part, update, precision=highest)
        return (memory, output)
    pieces = tuple((jnp.moveaxis(array, 2, 0) for array in (fading, solved_keys, solved_values, scores, carried, final_level)))
    initial = jnp.zeros((batch_size, head_count, key_dim, value_dim), queries.dtype)
    _, outputs = lax.scan(advance, initial, pieces)
    return jnp.moveaxis(outputs, 0, 2).reshape(batch_size, head_count, length, value_dim)

def token_mixer(projected, rate_logits, kernel, head_params, out_gain, segment):
    batch_size, length, _ = projected.shape
    head_count = head_params.shape[1]
    value_dim = out_gain.shape[0]
    channels = kernel.shape[1]
    key_width = (channels - head_count * value_dim) // 2
    key_dim = key_width // head_count
    mixed = short_conv(projected[..., :channels], kernel, segment)

    def heads_of(array, size):
        return jnp.moveaxis(array.reshape(batch_size, length, head_count, size), 2, 1)
    queries = heads_of(mixed[..., :key_width], key_dim)
    key_rows = heads_of(mixed[..., key_width:2 * key_width], key_dim)
    value_rows = heads_of(mixed[..., 2 * key_width:], value_dim)
    queries = queries * lax.rsqrt(lax.optimization_barrier(jnp.sum(queries * queries, -1, keepdims=True)) + 1e-06) * key_dim ** (-0.5)
    key_rows = key_rows * lax.rsqrt(lax.optimization_barrier(jnp.sum(key_rows * key_rows, -1, keepdims=True)) + 1e-06)
    beta_gate = jax.nn.sigmoid(jnp.moveaxis(rate_logits[..., head_count:], 2, 1))
    decays = -jnp.exp(head_params[0])[:, None] * jax.nn.softplus(jnp.moveaxis(rate_logits[..., :head_count], 2, 1) + head_params[1][:, None])
    earlier = jnp.pad(segment, ((0, 0), (1, 0)), constant_values=-1)[:, :length]
    decays = jnp.where((earlier != segment)[:, None, :], reset_level, decays)
    output = delta_rule(queries, key_rows, value_rows, beta_gate, decays, SPAN)
    output = output * lax.rsqrt(lax.optimization_barrier(jnp.mean(output * output, -1, keepdims=True)) + 1e-05) * out_gain
    gating = heads_of(projected[..., channels:], value_dim)
    return jnp.moveaxis(output * jax.nn.silu(gating), 1, 2).reshape(batch_size, length, head_count * value_dim)

def last_contract(left, right):
    return lax.dot_general(left.astype(jnp.float32), right.astype(jnp.float32), (((2,), (1,)), ((), ())), preferred_element_type=jnp.float32)

def layer_forward(entering, segment, weights, small_params):
    norm_gains, proj_weight, rate_weight, out_weight, up_weight, down_weight = weights
    kernel, head_params, out_gain = small_params
    widened = entering.astype(jnp.float32)
    normed_one, norm_one_back = jax.vjp(rms_gain, widened, norm_gains[0].astype(jnp.float32))
    hidden_one = normed_one.astype(jnp.bfloat16)
    projected = jnp.dot(hidden_one.astype(jnp.float32), proj_weight.astype(jnp.float32), preferred_element_type=jnp.float32)
    rate_logits = jnp.dot(hidden_one.astype(jnp.float32), rate_weight.astype(jnp.float32), preferred_element_type=jnp.float32)
    mixed_out, mixer_back = jax.vjp(partial(token_mixer, segment=segment), projected, rate_logits, kernel, head_params, out_gain)
    mixed_half = mixed_out.astype(jnp.bfloat16)
    stream = widened + last_contract(mixed_half, out_weight)
    normed_two, norm_two_back = jax.vjp(rms_gain, stream, norm_gains[1].astype(jnp.float32))
    hidden_two = normed_two.astype(jnp.bfloat16)
    gate_up = jnp.dot(hidden_two.astype(jnp.float32), up_weight.astype(jnp.float32), preferred_element_type=jnp.float32)
    activated, act_back = jax.vjp(swiglu, gate_up)
    act_half = activated.astype(jnp.bfloat16)
    layer_out = (stream + last_contract(act_half, down_weight)).astype(jnp.bfloat16)
    residuals = (norm_one_back, hidden_one, mixer_back, mixed_half, norm_two_back, hidden_two, act_back, act_half)
    return (layer_out, residuals)

def layer_backward(cotangent_in, residuals, weights):
    norm_gains, proj_weight, rate_weight, out_weight, up_weight, down_weight = weights
    norm_one_back, hidden_one, mixer_back, mixed_half, norm_two_back, hidden_two, act_back, act_half = residuals
    dout_half = cotangent_in.astype(jnp.bfloat16)
    gate_up_grad, = act_back(jnp.dot(dout_half.astype(jnp.float32), down_weight.astype(jnp.float32), preferred_element_type=jnp.float32))
    gate_up_cot = gate_up_grad.astype(jnp.bfloat16)
    stream_grad, gain_two = norm_two_back(last_contract(gate_up_cot, up_weight))
    stream_grad = cotangent_in + stream_grad
    branch_cot = stream_grad.astype(jnp.bfloat16)
    proj_grad, rate_grad, kernel_grad, head_grad, out_gain_grad = mixer_back(jnp.dot(branch_cot.astype(jnp.float32), out_weight.astype(jnp.float32), preferred_element_type=jnp.float32))
    proj_cot = proj_grad.astype(jnp.bfloat16)
    rate_cot = rate_grad.astype(jnp.bfloat16)
    hidden_grad = last_contract(proj_cot, proj_weight) + last_contract(rate_cot, rate_weight)
    entry_grad, gain_one = norm_one_back(hidden_grad)
    pairs = (hidden_one, proj_cot, rate_cot, mixed_half, branch_cot, hidden_two, gate_up_cot, act_half, dout_half)
    return (stream_grad + entry_grad, pairs, (kernel_grad, head_grad, out_gain_grad), jnp.stack([gain_one, gain_two]))

def weight_terms(pairs, gain_sum, start, count):
    flattened = [member.reshape(-1, member.shape[-1]) for member in pairs]
    hidden_one, proj_cot, rate_cot, mixed_half, branch_cot, hidden_two, gate_up_cot, act_half, dout_half = flattened

    def rows_of(matrix):
        return lax.dynamic_slice_in_dim(matrix, start, count, 1)

    def product(left, right):
        return lax.dot_general(left.astype(jnp.float32), right.astype(jnp.float32), (((0,), (0,)), ((), ())), preferred_element_type=jnp.float32)
    own_hidden = rows_of(hidden_one)
    return jnp.concatenate([product(own_hidden, proj_cot), product(own_hidden, rate_cot), product(rows_of(branch_cot), mixed_half), product(rows_of(hidden_two), gate_up_cot), product(rows_of(dout_half), act_half), rows_of(gain_sum).T], 1)

def split_term(total, widths):
    pieces = []
    column = 0
    for width in widths:
        pieces.append(total[..., column:column + width])
        column = column + width
    return pieces

def reference(tokens, segments, cotangent, norm_gains, proj_weight, rate_weight, out_weight, up_weight, down_weight, conv_kernels, head_params, out_gain):

    def weights_of(index):
        return (norm_gains[index], proj_weight[index], rate_weight[index], out_weight[index], up_weight[index], down_weight[index])

    def small_of(index):
        return (conv_kernels[index], head_params[index], out_gain[index])
    row_count = proj_weight.shape[1]
    widths = [proj_weight.shape[2], rate_weight.shape[2], out_weight.shape[2], up_weight.shape[2], down_weight.shape[2], 2]
    term_width = sum(widths)

    def one_batch(carry, inputs):
        entering, segment, incoming = inputs
        middle, saved_zero = layer_forward(entering, segment, weights_of(0), small_of(0))
        leaving, saved_one = layer_forward(middle, segment, weights_of(1), small_of(1))
        grad_middle, pairs_one, small_one, gains_one = layer_backward(incoming, saved_one, weights_of(1))
        grad_entry, pairs_zero, small_zero, gains_zero = layer_backward(grad_middle, saved_zero, weights_of(0))
        terms = jnp.stack([weight_terms(pairs_zero, gains_zero, 0, row_count), weight_terms(pairs_one, gains_one, 0, row_count)])
        smalls = tuple((carry[1][i] + jnp.stack([small_zero[i], small_one[i]]) for i in range(3)))
        return ((carry[0] + terms, smalls), (jnp.stack([middle, leaving]), jnp.stack([grad_entry, grad_middle])))
    initial = (jnp.zeros((2, row_count, term_width), jnp.float32), (jnp.zeros(conv_kernels.shape, jnp.float32), jnp.zeros(head_params.shape, jnp.float32), jnp.zeros(out_gain.shape, jnp.float32)))
    final, stacked = lax.scan(one_batch, initial, (tokens, segments, cotangent))
    totals, smalls = final
    section_output = jnp.moveaxis(stacked[0], 1, 0)
    input_grad = jnp.moveaxis(stacked[1], 1, 0)
    pieces = split_term(totals, widths)
    gains_grad = jnp.transpose(pieces[5], (0, 2, 1))
    return (section_output, input_grad, gains_grad, pieces[0], pieces[1], pieces[2], pieces[3], pieces[4], smalls[0], smalls[1], smalls[2])
```

```python
from functools import partial

import jax
import jax.numpy as jnp
from jax import lax
from jax.sharding import PartitionSpec as P

SPAN = 64


highest = lax.Precision.HIGHEST
reset_level = -30.0


def passed_along(value, axis, steps):
    count = lax.axis_size(axis)
    leading, last = (max(0, -steps), min(count, count - steps))
    return lax.ppermute(value, axis, [(source, source + steps) for source in range(leading, last)])


def rms_gain(values, gain_vec):
    return values * lax.rsqrt(jnp.mean(values * values, -1, keepdims=True) + 1e-06) * gain_vec


def swiglu(joined):
    half_width = joined.shape[-1] // 2
    return jax.nn.silu(joined[..., :half_width]) * joined[..., half_width:]


def short_conv(raw_input, kernel, segment):
    length = raw_input.shape[1]
    tap_count = kernel.shape[0]
    total = raw_input * kernel[tap_count - 1]
    for offset in range(1, tap_count):
        shifted = jnp.pad(raw_input, ((0, 0), (offset, 0), (0, 0)))[:, :length]
        earlier = jnp.pad(segment, ((0, 0), (offset, 0)), constant_values=-1)[:, :length]
        total = (
            total
            + jnp.where((earlier == segment)[..., None], shifted, 0.0)
            * kernel[tap_count - 1 - offset]
        )
    return jax.nn.silu(total)


@jax.custom_vjp
def unit_solve(system, right_side):
    return unit_solve_forward(system, right_side)[0]


def unit_lower_inverse(system):
    size = system.shape[-1]
    places = jnp.arange(size)
    inverse = None
    half = 1
    while half < size:
        rows, columns = places[:, None] // half, places[None, :] // half
        joins = (rows % 2 == 1) & (columns == rows - 1)
        corner = jnp.where(joins, system, 0.0)
        if inverse is None:
            inverse = jnp.eye(size, dtype=system.dtype) - corner
        else:
            inner = jnp.matmul(corner, inverse, precision=highest)
            inverse = inverse - jnp.matmul(inverse, inner, precision=highest)
        half = half * 2
    return inverse


def unit_solve_forward(system, right_side):
    inverse = unit_lower_inverse(system)
    solved = jnp.matmul(inverse, right_side, precision=highest)
    return solved, (inverse, solved)


def unit_solve_backward(saved, cotangent):
    inverse, solved = saved
    right_cot = jnp.matmul(jnp.swapaxes(inverse, -1, -2), cotangent, precision=highest)
    return -jnp.matmul(right_cot, jnp.swapaxes(solved, -1, -2), precision=highest), right_cot


unit_solve.defvjp(unit_solve_forward, unit_solve_backward)


def delta_rule(queries, key_rows, value_rows, beta_gate, decays, block_len):
    batch_size, head_count, length, key_dim = queries.shape
    value_dim = value_rows.shape[-1]
    block_count = length // block_len

    def to_blocks(array):
        return array.reshape(array.shape[:2] + (block_count, block_len) + array.shape[3:])

    queries = to_blocks(queries)
    key_rows = to_blocks(key_rows)
    value_rows = to_blocks(value_rows)
    beta_gate = to_blocks(beta_gate)
    levels = jnp.cumsum(to_blocks(decays), axis=-1)
    places = jnp.arange(block_len)
    lower_mask = places[:, None] >= places[None, :]
    strict_mask = places[:, None] > places[None, :]
    spread = jnp.exp(jnp.where(lower_mask, levels[..., :, None] - levels[..., None, :], -1e30))
    beta_keys = key_rows * beta_gate[..., None]
    key_inner = jnp.einsum("bhncd,bhnmd->bhncm", beta_keys, key_rows, precision=highest) * spread
    system = jnp.where(strict_mask, key_inner, 0.0)
    right_side = jnp.concatenate(
        [beta_keys * jnp.exp(levels)[..., None], value_rows * beta_gate[..., None]], -1
    )
    solved = unit_solve(system, right_side)
    solved_keys = solved[..., :key_dim]
    solved_values = solved[..., key_dim:]
    scores = jnp.einsum("bhncd,bhnmd->bhncm", queries, key_rows, precision=highest) * spread
    fading = queries * jnp.exp(levels)[..., None]
    final_level = levels[..., -1:]
    carried = key_rows * jnp.exp(final_level - levels)[..., None]

    def advance(memory, pieces):
        fading_part, keys_part, values_part, scores_part, carried_part, final_part = pieces
        update = values_part - jnp.einsum("bhcd,bhde->bhce", keys_part, memory, precision=highest)
        output = jnp.einsum("bhcd,bhde->bhce", fading_part, memory, precision=highest) + jnp.einsum(
            "bhcm,bhme->bhce", scores_part, update, precision=highest
        )
        memory = memory * jnp.exp(final_part)[..., None] + jnp.einsum(
            "bhcd,bhce->bhde", carried_part, update, precision=highest
        )
        return (memory, output)

    pieces = tuple(
        (
            jnp.moveaxis(array, 2, 0)
            for array in (fading, solved_keys, solved_values, scores, carried, final_level)
        )
    )
    initial = jnp.zeros((batch_size, head_count, key_dim, value_dim), queries.dtype)
    _, outputs = lax.scan(advance, initial, pieces, unroll=block_count)
    return jnp.moveaxis(outputs, 0, 2).reshape(batch_size, head_count, length, value_dim)


def token_mixer(projected, rate_logits, kernel, head_params, out_gain, segment):
    batch_size, length, _ = projected.shape
    head_count = head_params.shape[1]
    value_dim = out_gain.shape[0]
    channels = kernel.shape[1]
    key_width = (channels - head_count * value_dim) // 2
    key_dim = key_width // head_count
    mixed = short_conv(projected[..., :channels], kernel, segment)

    def heads_of(array, size):
        return jnp.moveaxis(array.reshape(batch_size, length, head_count, size), 2, 1)

    queries = heads_of(mixed[..., :key_width], key_dim)
    key_rows = heads_of(mixed[..., key_width : 2 * key_width], key_dim)
    value_rows = heads_of(mixed[..., 2 * key_width :], value_dim)
    queries = (
        queries
        * lax.rsqrt(jnp.sum(queries * queries, -1, keepdims=True) + 1e-06)
        * key_dim ** (-0.5)
    )
    key_rows = key_rows * lax.rsqrt(jnp.sum(key_rows * key_rows, -1, keepdims=True) + 1e-06)
    beta_gate = jax.nn.sigmoid(jnp.moveaxis(rate_logits[..., head_count:], 2, 1))
    decays = -jnp.exp(head_params[0])[:, None] * jax.nn.softplus(
        jnp.moveaxis(rate_logits[..., :head_count], 2, 1) + head_params[1][:, None]
    )
    earlier = jnp.pad(segment, ((0, 0), (1, 0)), constant_values=-1)[:, :length]
    decays = jnp.where((earlier != segment)[:, None, :], reset_level, decays)
    output = delta_rule(queries, key_rows, value_rows, beta_gate, decays, SPAN)
    output = output * lax.rsqrt(jnp.mean(output * output, -1, keepdims=True) + 1e-05) * out_gain
    gating = heads_of(projected[..., channels:], value_dim)
    return jnp.moveaxis(output * jax.nn.silu(gating), 1, 2).reshape(
        batch_size, length, head_count * value_dim
    )


def last_contract(left, right):
    return lax.dot_general(
        left, right, (((2,), (1,)), ((), ())), preferred_element_type=jnp.float32
    )


def layer_forward(entering, segment, weights, small_params):
    norm_gains, first_weight, out_weight, up_weight, down_weight = weights
    kernel, head_params, out_gain = small_params
    widened = entering.astype(jnp.float32)
    normed_one, norm_one_back = jax.vjp(rms_gain, widened, norm_gains[0].astype(jnp.float32))
    hidden_one = normed_one.astype(jnp.bfloat16)
    joined = jnp.dot(hidden_one, first_weight, preferred_element_type=jnp.float32)
    rates = 2 * head_params.shape[1]
    proj_width = kernel.shape[1] + head_params.shape[1] * out_gain.shape[0]
    projected = joined[..., :proj_width]
    rate_logits = joined[..., proj_width : proj_width + rates]
    mixed_out, mixer_back = jax.vjp(
        partial(token_mixer, segment=segment), projected, rate_logits, kernel, head_params, out_gain
    )
    mixed_half = mixed_out.astype(jnp.bfloat16)
    stream = widened + last_contract(mixed_half, out_weight)
    normed_two, norm_two_back = jax.vjp(rms_gain, stream, norm_gains[1].astype(jnp.float32))
    hidden_two = normed_two.astype(jnp.bfloat16)
    gate_up = jnp.dot(hidden_two, up_weight, preferred_element_type=jnp.float32)
    activated, act_back = jax.vjp(swiglu, gate_up)
    act_half = activated.astype(jnp.bfloat16)
    layer_out = (stream + last_contract(act_half, down_weight)).astype(jnp.bfloat16)
    residuals = (
        norm_one_back,
        hidden_one,
        mixer_back,
        mixed_half,
        norm_two_back,
        hidden_two,
        act_back,
        act_half,
    )
    return (layer_out, residuals)


def layer_backward(cotangent_in, residuals, weights):
    norm_gains, first_weight, out_weight, up_weight, down_weight = weights
    (
        norm_one_back,
        hidden_one,
        mixer_back,
        mixed_half,
        norm_two_back,
        hidden_two,
        act_back,
        act_half,
    ) = residuals
    dout_half = cotangent_in.astype(jnp.bfloat16)
    (gate_up_grad,) = act_back(jnp.dot(dout_half, down_weight, preferred_element_type=jnp.float32))
    gate_up_cot = gate_up_grad.astype(jnp.bfloat16)
    stream_grad, gain_two = norm_two_back(last_contract(gate_up_cot, up_weight))
    stream_grad = cotangent_in + stream_grad
    branch_cot = stream_grad.astype(jnp.bfloat16)
    proj_grad, rate_grad, kernel_grad, head_grad, out_gain_grad = mixer_back(
        jnp.dot(branch_cot, out_weight, preferred_element_type=jnp.float32)
    )
    proj_cot = proj_grad.astype(jnp.bfloat16)
    rate_cot = rate_grad.astype(jnp.bfloat16)
    used = proj_cot.shape[-1] + rate_cot.shape[-1]
    spare = jnp.zeros(proj_cot.shape[:-1] + (first_weight.shape[1] - used,), jnp.bfloat16)
    first_cot = jnp.concatenate([proj_cot, rate_cot, spare], -1)
    hidden_grad = last_contract(first_cot, first_weight)
    entry_grad, gain_one = norm_one_back(hidden_grad)
    pairs = (
        hidden_one,
        first_cot,
        mixed_half,
        branch_cot,
        hidden_two,
        gate_up_cot,
        act_half,
        dout_half,
    )
    return (
        stream_grad + entry_grad,
        pairs,
        (kernel_grad, head_grad, out_gain_grad),
        jnp.stack([gain_one, gain_two]),
    )


def weight_terms(pairs, gain_sum):
    flattened = [member.reshape(-1, member.shape[-1]) for member in pairs]
    (
        hidden_one,
        first_cot,
        mixed_half,
        branch_cot,
        hidden_two,
        gate_up_cot,
        act_half,
        dout_half,
    ) = flattened

    def product(left, right):
        return lax.dot_general(
            left, right, (((0,), (0,)), ((), ())), preferred_element_type=jnp.float32
        )

    first = product(hidden_one, first_cot)
    first = jnp.concatenate([first[:, : -gain_sum.shape[0]], gain_sum.T], 1)
    return (
        product(dout_half, act_half),
        product(hidden_two, gate_up_cot),
        product(branch_cot, mixed_half),
        first,
    )


group = ("fsdp", "dp")


def gathered(shard):
    count = shard.shape[0] // lax.axis_size("dp")
    part = lax.dynamic_slice_in_dim(shard, lax.axis_index("dp") * count, count, 0)
    return lax.all_gather(part, group, axis=0, tiled=True)


def scattered(term):
    part = lax.psum_scatter(term.astype(jnp.bfloat16), group, scatter_dimension=0, tiled=True)
    return lax.all_gather(part, "dp", axis=0, tiled=True).astype(jnp.float32)


def summed_small(arrays):
    flat = jnp.concatenate([array.reshape(-1) for array in arrays])
    padded = jnp.pad(flat, (0, -flat.size % 1024)).reshape(-1, 128)
    members = lax.all_gather(padded, group, axis=0, tiled=True)
    total = jnp.sum(members.reshape((-1,) + padded.shape), 0).reshape(-1)
    pieces = []
    place = 0
    for array in arrays:
        pieces.append(total[place : place + array.size].reshape(array.shape))
        place = place + array.size
    return pieces


def pass_forward(layer_out):
    return passed_along(layer_out, "section", 1)


def pass_backward(entry_grad):
    return passed_along(entry_grad.astype(jnp.bfloat16), "section", -1).astype(entry_grad.dtype)


def shards(
    tokens,
    segments,
    cotangent,
    norm_gains,
    proj_weight,
    rate_weight,
    out_weight,
    up_weight,
    down_weight,
    conv_kernels,
    head_params,
    out_gain,
):
    first_section = lax.axis_index("section") == 0
    first_weight = gathered(
        jnp.concatenate([proj_weight[0], rate_weight[0], norm_gains[0].T], 1)
    )
    weights = (
        first_weight[:, -norm_gains.shape[1] :].T,
        first_weight,
        gathered(out_weight[0]),
        gathered(up_weight[0]),
        gathered(down_weight[0]),
    )
    small_params = (conv_kernels[0], head_params[0], out_gain[0])
    batches = tokens.shape[0]
    records = []
    results = []
    for forward_step in range(batches + 1):
        ahead_batch = min(forward_step, batches - 1)
        behind = max(forward_step - 1, 0)
        segment = jnp.where(first_section, segments[ahead_batch], segments[behind])
        if forward_step == 0:
            entering = tokens[0]
        else:
            entering = jnp.where(first_section, tokens[ahead_batch], pass_forward(results[-1]))
        produced, residuals = layer_forward(entering, segment, weights, small_params)
        records.append(residuals)
        results.append(produced)
    incoming = []
    kept_pairs = []
    small_list = []
    gain_list = []
    for backward_step in range(batches + 1):
        if backward_step < batches:
            own_cot = cotangent[batches - 1 - backward_step]
        else:
            own_cot = jnp.zeros_like(cotangent[0])
        if backward_step == 0:
            upstream = jnp.zeros_like(own_cot)
        else:
            upstream = pass_backward(incoming[-1])
        dout_full = jnp.where(first_section, upstream, own_cot)
        entry_grad, pairs, small_grads, gains_step = layer_backward(
            dout_full, records[batches - backward_step], weights
        )
        incoming.append(entry_grad)
        kept_pairs.append(pairs)
        small_list.append(small_grads)
        gain_list.append(gains_step)
    if batches == 1:
        pairs_all = tuple((jnp.where(first_section, b, a) for a, b in zip(*kept_pairs)))
    else:
        pairs_all = tuple((jnp.concatenate(members, 1) for members in zip(*kept_pairs)))
    gain_sum = sum(gain_list)
    small_sum = tuple((sum((member[i] for member in small_list)) for i in range(3)))
    section_output = jnp.stack([jnp.where(first_section, results[0], results[1])])[None]
    input_grad = jnp.stack([jnp.where(first_section, incoming[batches], incoming[batches - 1])])[
        None
    ]
    down_grad, up_grad, out_grad, first_grad = map(scattered, weight_terms(pairs_all, gain_sum))
    kernel_grad, head_grad, out_gain_grad = summed_small(small_sum)
    proj_width = proj_weight.shape[2]
    used = proj_width + rate_weight.shape[2]
    return (
        section_output,
        input_grad,
        first_grad[:, used:].T[None],
        first_grad[:, :proj_width][None],
        first_grad[:, proj_width:used][None],
        out_grad[None],
        up_grad[None],
        down_grad[None],
        kernel_grad[None],
        head_grad[None],
        out_gain_grad[None],
    )


def solution(mesh):
    return jax.shard_map(
        shards,
        mesh=mesh,
        in_specs=(
            P(None, ("fsdp", "dp"), None, None),
            P(None, ("fsdp", "dp"), None),
            P(None, ("fsdp", "dp"), None, None),
            P("section", None, "fsdp"),
            P("section", "fsdp", None),
            P("section", "fsdp", None),
            P("section", "fsdp", None),
            P("section", "fsdp", None),
            P("section", "fsdp", None),
            P("section", None, None),
            P("section", None, None),
            P("section", None),
        ),
        out_specs=(
            P("section", None, ("fsdp", "dp"), None, None),
            P("section", None, ("fsdp", "dp"), None, None),
            P("section", None, "fsdp"),
            P("section", "fsdp", None),
            P("section", "fsdp", None),
            P("section", "fsdp", None),
            P("section", "fsdp", None),
            P("section", "fsdp", None),
            P("section", None, None),
            P("section", None, None),
            P("section", None),
        ),
        check_vma=False,
    )
```
